256 devices in a mesh: seq: 32 (over z, y), tp: 8 (over x, core).
Axes of the slice: x: 4, y: 4, z: 8, core: 2. Of those that a mesh axis runs over, the one named last changes fastest.
Arguments:
- query_raw: bfloat16 [16384, 4096], P('seq', 'tp'), may hold values from -6 to 6
- key_raw: bfloat16 [16384, 4096], P('seq', 'tp'), may hold values from -6 to 6
- value_raw: bfloat16 [16384, 4096], P('seq', 'tp'), may hold values from -6 to 6
- conv_taps: float32 [3, 4, 4096], P(None, None, 'tp'), may hold values from -3 to 3
- layout_boxes: int32 [4, 16384], P(None, 'seq'), may hold values from 0 to 1023
- box_tables: bfloat16 [2, 1024, 4096], P(None, None, 'tp'), may hold values from -4 to 4
- log_decay: float32 [32, 16384], P('tp', 'seq'), may hold values from -1 to 0, as said below
- norm_gain: float32 [4096], P('tp'), may hold values from 0.25 to 1.75
- out_weight: bfloat16 [4096, 4096], P('tp', 'seq'), may hold values from -0.09375 to 0.09375
- grad_output: bfloat16 [16384, 4096], P('seq', 'tp'), may hold values from -6 to 6
Outputs:
- layer_out: bfloat16 [16384, 4096], P('seq', 'tp')
- grad_query: bfloat16 [16384, 4096], P('seq', 'tp')
- grad_key: bfloat16 [16384, 4096], P('seq', 'tp')
- grad_value: bfloat16 [16384, 4096], P('seq', 'tp')
- grad_taps: float32 [3, 4, 4096], P(None, None, 'tp')
- grad_tables: float32 [2, 1024, 4096], P(None, None, 'tp')
- grad_gain: float32 [4096], P('tp')
- grad_weight: float32 [4096, 4096], P('tp', 'seq')
The draws below stay inside these ranges and needn't reach their ends.
Inputs may be any that keep to these rules, and one draw needn't show every extreme that they name: `log_decay`: each entry is the logarithm (at most 0) of one head's state decay at one token.
All inputs are finite; a program needn't handle non-finite values.
Results may differ from the reference program's by a relative error of at most 0.02.
Values may be sent and summed in bfloat16 or wider, within the bound.
A program may use at most 128 MiB of HBM per device.

```python
import math
import jax
import jax.numpy as jnp
from jax import lax

HEAD_TOTAL = 32
DH = 128
D = 4096
KW = 4
NB = 1024
TOK_DEV = 512
TOKEN_TOTAL = 16384
N_SEQ = 32
N_TP = 8


def draw_log_decay(key, part):
    key_vectors = jax.random.split(key, 8)
    ranking = jax.random.permutation(key_vectors[0], HEAD_TOTAL)
    slow_heads = ranking >= HEAD_TOTAL // 2
    fast_heads = ranking < HEAD_TOTAL // 4
    jitter = jnp.exp(jax.random.uniform(key_vectors[3], (HEAD_TOTAL, TOKEN_TOTAL), minval=math.log(0.5), maxval=math.log(1.5)))
    fast_rate = 1.0 / jax.random.uniform(key_vectors[1], (HEAD_TOTAL,), minval=30.0, maxval=50.0)
    block_keep = jnp.exp(jax.random.uniform(key_vectors[7], (HEAD_TOTAL,), minval=math.log(0.2), maxval=math.log(0.8)))
    middle_rate = -jnp.log(block_keep) / TOK_DEV
    slow_rate = jax.random.uniform(key_vectors[2], (HEAD_TOTAL,), minval=0.5, maxval=1.5) / TOKEN_TOTAL
    rate = jnp.where(slow_heads, slow_rate, jnp.where(fast_heads, fast_rate, middle_rate))
    block_factor = jnp.exp(jax.random.uniform(key_vectors[4], (HEAD_TOTAL, TOKEN_TOTAL // TOK_DEV), minval=math.log(0.5), maxval=math.log(1.5)))
    block_factor = jnp.repeat(block_factor, TOK_DEV, axis=1)
    spike_locations = jax.random.randint(key_vectors[5], (3,), 0, TOKEN_TOTAL)
    spike_contact = jnp.any(jnp.arange(TOKEN_TOTAL)[None, :] == spike_locations[:, None], axis=0)
    spike_removal = jnp.log(jax.random.uniform(key_vectors[6], (HEAD_TOTAL, TOKEN_TOTAL), minval=0.6, maxval=0.8))
    value_vectors = -rate[:, None] * jitter * block_factor
    value_vectors = value_vectors + jnp.where(spike_contact[None, :] & slow_heads[:, None], spike_removal, 0.0)
    return value_vectors.astype(jnp.float32)


def touch_ends(values, key, low, high):
    longest = values.shape.index(max(values.shape))
    spots = []
    for shift in (0, 1):
        where = [jax.random.randint(jax.random.fold_in(key, axis), (), 0, length) for axis, length in enumerate(values.shape)]
        where[longest] = (where[longest] + shift) % values.shape[longest]
        spots.append(tuple(where))
    return values.at[spots[0]].set(low).at[spots[1]].set(high)


def raised(array, stream_key, source, target, shards_of, factor):
    owner, partner = [(jnp.arange(array.shape[axis_at]) // (array.shape[axis_at] // shards_of)).reshape([-1 if axis == axis_at else 1 for axis in range(array.ndim)]) for axis_at in (source, target)]
    chosen = jax.random.permutation(stream_key, shards_of)[partner]
    strong = (owner == chosen) | (owner == (partner + shards_of // 2) % shards_of)
    return jnp.where(strong, factor * array, array)


def block_scale(rng, dims, shards, smallest, high):
    def one(position, shards_of):
        heights = jax.random.uniform(jax.random.fold_in(jax.random.fold_in(rng, 6), position), (shards_of,), jnp.float32, smallest / len(shards), high / len(shards))
        return jnp.repeat(jnp.exp(heights), dims[position] // shards_of).reshape((-1,) + (1,) * (len(dims) - position - 1))

    loudness = one(*shards[0])
    for cut in shards[1:]:
        loudness = loudness * one(*cut)
    return loudness


def bell_draw(stream_key, shape, spread, most, shards=(), kind=jnp.bfloat16):
    factor_of = block_scale(stream_key, shape, shards, -0.22, 0.18) if shards else 1.0
    values = jax.random.normal(stream_key, shape, jnp.float32) * spread * factor_of
    return jnp.minimum(jnp.maximum(values, -most), most).astype(kind)


def gaussian_with(own_key, shape, deviation, limit, cuts, heavy, held_as=jnp.bfloat16):
    values = deviation * jax.random.normal(own_key, shape, jnp.float32)
    if cuts:
        values = values * block_scale(own_key, shape, cuts, -0.22, 0.18)
    return jnp.clip(raised(values, jax.random.fold_in(own_key, 3), *heavy), -limit, limit).astype(held_as)


def setup_inputs(seed: int = 0) -> dict:
    arg_keys = jax.random.split(jax.random.key(seed), 11)
    return {
        "query_raw": bell_draw(arg_keys[0], (TOKEN_TOTAL, D), 1.0, 6.0, ((0, 32), (1, 8))),
        "key_raw": bell_draw(arg_keys[1], (TOKEN_TOTAL, D), 1.0, 6.0, ((0, 32), (1, 8))),
        "value_raw": bell_draw(arg_keys[2], (TOKEN_TOTAL, D), 1.0, 6.0, ((0, 32), (1, 8))),
        "conv_taps": bell_draw(arg_keys[3], (3, KW, D), 0.5, 3.0, ((2, 8),), jnp.float32),
        "layout_boxes": touch_ends(jax.random.randint(arg_keys[4], (4, TOKEN_TOTAL), 0, NB), jax.random.fold_in(arg_keys[4], 1), 0, NB - 1).astype(jnp.int32),
        "box_tables": bell_draw(arg_keys[5], (2, NB, D), 0.25, 4.0, ((2, 8),)),
        "log_decay": draw_log_decay(jax.random.fold_in(arg_keys[10], 71), 0),
        "norm_gain": jnp.clip(1.0 + 0.15 * jax.random.normal(arg_keys[7], (D,), jnp.float32), 0.25, 1.75),
        "out_weight": bell_draw(arg_keys[8], (D, D), D ** -0.5, 0.09375, ((0, 8), (1, 32))),
        "grad_output": gaussian_with(arg_keys[9], (TOKEN_TOTAL, D), 1.0, 6.0, ((0, 32), (1, 8)), (0, 1, 32, 2.75)),
    }


HIGHEST = lax.Precision.HIGHEST

def causal_conv(signal, taps):
    length = signal.shape[0]
    padded = jnp.concatenate([jnp.zeros((KW - 1, signal.shape[1]), jnp.float32), signal], axis=0)
    result = jnp.zeros_like(signal)
    for tap_step in range(KW):
        result = result + taps[tap_step] * padded[KW - 1 - tap_step:KW - 1 - tap_step + length]
    return (result, padded)

def conv_adjoint(grad, taps):
    length = grad.shape[0]
    extended = jnp.concatenate([grad, jnp.zeros((KW - 1, grad.shape[1]), jnp.float32)], axis=0)
    result = jnp.zeros_like(grad)
    for tap_step in range(KW):
        result = result + taps[tap_step] * extended[tap_step:tap_step + length]
    return result

def tap_grads(grad, padded):
    length = grad.shape[0]
    return jnp.stack([lax.optimization_barrier(jnp.sum(grad * padded[KW - 1 - tap_step:KW - 1 - tap_step + length], axis=0)) for tap_step in range(KW)])

def to_blocks(matrix):
    return matrix.astype(jnp.float32).reshape(N_SEQ, TOK_DEV, HEAD_TOTAL, DH).transpose(0, 2, 1, 3)

def from_blocks(blocks):
    return blocks.transpose(0, 2, 1, 3).reshape(N_SEQ * TOK_DEV, D)

def reference(query_raw, key_raw, value_raw, conv_taps, layout_boxes, box_tables, log_decay, norm_gain, out_weight, grad_output):
    feature_scale = DH ** (-0.5)
    bucket_ids = jnp.arange(NB, dtype=jnp.int32)

    def count_table(first, second):
        return (first[:, None] == bucket_ids[None, :]).astype(jnp.bfloat16) + (second[:, None] == bucket_ids[None, :]).astype(jnp.bfloat16)
    hot_x = count_table(layout_boxes[0], layout_boxes[2])
    hot_y = count_table(layout_boxes[1], layout_boxes[3])
    layout = jnp.dot(hot_x, box_tables[0], preferred_element_type=jnp.float32) + jnp.dot(hot_y, box_tables[1], preferred_element_type=jnp.float32)
    conv_query, pad_query = causal_conv(query_raw.astype(jnp.float32), conv_taps[0])
    conv_key, pad_key = causal_conv(key_raw.astype(jnp.float32), conv_taps[1])
    conv_value, pad_value = causal_conv(value_raw.astype(jnp.float32), conv_taps[2])
    query_feat = (feature_scale * (conv_query + layout)).astype(jnp.bfloat16)
    key_feat = (conv_key + layout).astype(jnp.bfloat16)
    value_feat = conv_value.astype(jnp.bfloat16)
    query_blocks = to_blocks(query_feat)
    key_blocks = to_blocks(key_feat)
    value_blocks = to_blocks(value_feat)
    decay_sum = jnp.cumsum(log_decay.reshape(HEAD_TOTAL, N_SEQ, TOK_DEV).transpose(1, 0, 2), axis=2)
    positions = jnp.arange(TOK_DEV, dtype=jnp.int32)
    causal_mask = positions[:, None] >= positions[None, :]

    def decay_weights(block_sum):
        return jnp.where(causal_mask[None], jnp.exp(jnp.minimum(block_sum[:, :, None] - block_sum[:, None, :], 0.0)), 0.0)

    def forward_block(state, inputs):
        query_b, key_b, value_b, block_sum = inputs
        decay_total = block_sum[:, -1]
        scores = decay_weights(block_sum) * jnp.einsum('hti,hsi->hts', query_b, key_b, precision=HIGHEST)
        attended = jnp.einsum('hts,hsj->htj', scores, value_b, precision=HIGHEST)
        attended = attended + jnp.exp(block_sum)[:, :, None] * jnp.einsum('hti,hij->htj', query_b, state, precision=HIGHEST)
        local_state = jnp.einsum('hsi,hsj->hij', key_b * jnp.exp(decay_total[:, None] - block_sum)[:, :, None], value_b, precision=HIGHEST)
        return (jnp.exp(decay_total)[:, None, None] * state + local_state, (attended, state))
    start_state = jnp.zeros((HEAD_TOTAL, DH, DH), jnp.float32)
    _, (attended, incoming) = lax.scan(forward_block, start_state, (query_blocks, key_blocks, value_blocks, decay_sum))
    inverse = lax.rsqrt(lax.optimization_barrier(jnp.mean(attended * attended, axis=-1, keepdims=True)) + 1e-06)
    unit_norm = attended * inverse
    gain_heads = norm_gain.reshape(1, HEAD_TOTAL, 1, DH)
    normed = from_blocks(unit_norm * gain_heads).astype(jnp.bfloat16)
    group = D // N_TP
    layer_sum = jnp.zeros((N_SEQ * TOK_DEV, D), jnp.float32)
    for group_index in range(N_TP):
        partial_sum = jnp.dot(normed[:, group_index * group:(group_index + 1) * group], out_weight[group_index * group:(group_index + 1) * group], preferred_element_type=jnp.float32)
        layer_sum = layer_sum + lax.optimization_barrier(partial_sum.astype(jnp.bfloat16)).astype(jnp.float32)
    layer_out = layer_sum.astype(jnp.bfloat16)
    grad_normed = jnp.dot(grad_output, out_weight.T, preferred_element_type=jnp.float32).astype(jnp.bfloat16)
    grad_weight = jnp.dot(normed.T, grad_output, preferred_element_type=jnp.float32)
    grad_blocks = to_blocks(grad_normed)
    grad_gain = lax.optimization_barrier(jnp.sum(grad_blocks * unit_norm, axis=(0, 2))).reshape(D)
    grad_unit = grad_blocks * gain_heads
    grad_attended = inverse * (grad_unit - unit_norm * lax.optimization_barrier(jnp.mean(grad_unit * unit_norm, axis=-1, keepdims=True)))

    def backward_block(state, inputs):
        query_b, key_b, value_b, block_sum, grad_b, earlier_state = inputs
        decay_total = block_sum[:, -1]
        weights = decay_weights(block_sum)
        tail_decay = jnp.exp(decay_total[:, None] - block_sum)[:, :, None]
        head_decay = jnp.exp(block_sum)[:, :, None]
        scores = weights * jnp.einsum('hti,hsi->hts', query_b, key_b, precision=HIGHEST)
        grad_scores = weights * jnp.einsum('htj,hsj->hts', grad_b, value_b, precision=HIGHEST)
        grad_q = jnp.einsum('hts,hsi->hti', grad_scores, key_b, precision=HIGHEST) + head_decay * jnp.einsum('htj,hij->hti', grad_b, earlier_state, precision=HIGHEST)
        grad_k = jnp.einsum('hts,hti->hsi', grad_scores, query_b, precision=HIGHEST) + tail_decay * jnp.einsum('hsj,hij->hsi', value_b, state, precision=HIGHEST)
        grad_v = jnp.einsum('hts,htj->hsj', scores, grad_b, precision=HIGHEST) + tail_decay * jnp.einsum('hsi,hij->hsj', key_b, state, precision=HIGHEST)
        local_state = jnp.einsum('hti,htj->hij', query_b * head_decay, grad_b, precision=HIGHEST)
        return (jnp.exp(decay_total)[:, None, None] * state + local_state, (grad_q, grad_k, grad_v))
    _, (grad_qf, grad_kf, grad_vf) = lax.scan(backward_block, start_state, (query_blocks, key_blocks, value_blocks, decay_sum, grad_attended, incoming), reverse=True)
    grad_pre_q = feature_scale * from_blocks(grad_qf)
    grad_pre_k = from_blocks(grad_kf)
    grad_pre_v = from_blocks(grad_vf)
    grad_query = conv_adjoint(grad_pre_q, conv_taps[0]).astype(jnp.bfloat16)
    grad_key = conv_adjoint(grad_pre_k, conv_taps[1]).astype(jnp.bfloat16)
    grad_value = conv_adjoint(grad_pre_v, conv_taps[2]).astype(jnp.bfloat16)
    grad_taps = jnp.stack([tap_grads(grad_pre_q, pad_query), tap_grads(grad_pre_k, pad_key), tap_grads(grad_pre_v, pad_value)])
    grad_layout = (grad_pre_q + grad_pre_k).astype(jnp.bfloat16)
    grad_tables = jnp.stack([jnp.dot(hot_x.T, grad_layout, preferred_element_type=jnp.float32), jnp.dot(hot_y.T, grad_layout, preferred_element_type=jnp.float32)])
    return (layer_out, grad_query, grad_key, grad_value, grad_taps, grad_tables, grad_gain, grad_weight)
```

```python
import jax
import jax.numpy as jnp
from jax import lax
from jax.sharding import PartitionSpec as P

HIGHEST = lax.Precision.HIGHEST


def shifted(x, axis, by):
    length = lax.axis_size(axis)
    pairs = [(i, i + by) for i in range(length) if 0 <= i + by < length]
    return lax.ppermute(x, axis, pairs)


def entering(log_total, state, axis, reverse):
    length = lax.axis_size(axis)
    step = -1 if reverse else 1
    log_total, state = shifted((log_total, state), axis, step)
    distance = 1
    while distance < length:
        far_total, far_state = shifted((log_total, state), axis, step * distance)
        state = jnp.exp(log_total)[:, None, None] * far_state + state
        log_total = far_total + log_total
        distance *= 2
    return state


def on_device(
    query_raw,
    key_raw,
    value_raw,
    conv_taps,
    layout_boxes,
    box_tables,
    log_decay,
    norm_gain,
    out_weight,
    grad_output,
):
    row_count, feat_width = query_raw.shape
    head_count = log_decay.shape[0]
    head_size = feat_width // head_count
    kernel = conv_taps.shape[1]
    buckets = box_tables.shape[1]
    feature_scale = head_size ** (-0.5)
    stacked = jnp.stack([query_raw, key_raw, value_raw])
    rim_rows = shifted(stacked[:, row_count - (kernel - 1) :, :], "seq", 1)
    padded = jnp.concatenate([rim_rows, stacked], axis=1).astype(jnp.float32)
    conved = jnp.zeros((3, row_count, feat_width), jnp.float32)
    for tap_step in range(kernel):
        conved = (
            conved
            + conv_taps[:, tap_step, None, :]
            * padded[:, kernel - 1 - tap_step : kernel - 1 - tap_step + row_count, :]
        )
    bucket_ids = jnp.arange(buckets, dtype=jnp.int32)

    def count_table(first, second):
        return (first[:, None] == bucket_ids[None, :]).astype(jnp.bfloat16) + (
            second[:, None] == bucket_ids[None, :]
        ).astype(jnp.bfloat16)

    hot_x = count_table(layout_boxes[0], layout_boxes[2])
    hot_y = count_table(layout_boxes[1], layout_boxes[3])
    layout = jnp.dot(hot_x, box_tables[0], preferred_element_type=jnp.float32) + jnp.dot(
        hot_y, box_tables[1], preferred_element_type=jnp.float32
    )
    query_feat = (feature_scale * (conved[0] + layout)).astype(jnp.bfloat16)
    key_feat = (conved[1] + layout).astype(jnp.bfloat16)
    value_feat = conved[2].astype(jnp.bfloat16)

    def split_heads(matrix):
        return matrix.reshape(row_count, head_count, head_size).transpose(1, 0, 2)

    def join_heads(blocks):
        return blocks.transpose(1, 0, 2).reshape(row_count, feat_width)

    query_heads = split_heads(query_feat)
    key_heads = split_heads(key_feat)
    value_heads = split_heads(value_feat)
    decay_sum = jnp.cumsum(log_decay, axis=1)
    decay_total = decay_sum[:, -1]
    head_decay = jnp.exp(decay_sum)[:, :, None]
    tail_decay = jnp.exp(decay_total[:, None] - decay_sum)[:, :, None]
    positions = jnp.arange(row_count, dtype=jnp.int32)
    causal_mask = positions[:, None] >= positions[None, :]
    decay_mask = jnp.where(
        causal_mask[None],
        jnp.exp(jnp.minimum(decay_sum[:, :, None] - decay_sum[:, None, :], 0.0)),
        0.0,
    )
    local_state = jnp.einsum("hsi,hsj->hij", key_heads * tail_decay, value_heads, precision=HIGHEST)
    incoming = entering(decay_total, local_state, "seq", False)
    scores = decay_mask * jnp.einsum(
        "hti,hsi->hts", query_heads, key_heads, preferred_element_type=jnp.float32
    )
    attended = jnp.einsum("hts,hsj->htj", scores, value_heads, precision=HIGHEST)
    attended = attended + head_decay * jnp.einsum(
        "hti,hij->htj", query_heads, incoming, precision=HIGHEST
    )
    inverse = lax.rsqrt(jnp.mean(attended * attended, axis=-1, keepdims=True) + 1e-06)
    unit_norm = attended * inverse
    gain_heads = norm_gain.reshape(head_count, 1, head_size)
    normed = join_heads(unit_norm * gain_heads).astype(jnp.bfloat16)
    partial_sum = jnp.dot(
        normed,
        lax.all_gather(out_weight, "seq", axis=1, tiled=True),
        preferred_element_type=jnp.float32,
    )
    layer_out = lax.psum_scatter(
        partial_sum.astype(jnp.bfloat16), "tp", scatter_dimension=1, tiled=True
    )
    cotangent = lax.all_gather(grad_output, "tp", axis=1, tiled=True)
    contract_last = (((1,), (1,)), ((), ()))
    grad_normed_sum = lax.dot_general(
        cotangent,
        lax.all_gather(out_weight, "seq", axis=1, tiled=True),
        contract_last,
        preferred_element_type=jnp.float32,
    )
    grad_normed = grad_normed_sum.astype(jnp.bfloat16)
    contract_first = (((0,), (0,)), ((), ()))
    weight_terms = lax.dot_general(
        normed, cotangent, contract_first, preferred_element_type=jnp.float32
    )
    grad_weight = lax.psum_scatter(
        weight_terms.astype(jnp.bfloat16), "seq", scatter_dimension=1, tiled=True
    ).astype(jnp.float32)
    grad_heads = split_heads(grad_normed).astype(jnp.float32)
    gain_terms = jnp.sum(grad_heads * unit_norm, axis=1).reshape(feat_width)
    grad_unit = grad_heads * gain_heads
    grad_attended = inverse * (
        grad_unit - unit_norm * jnp.mean(grad_unit * unit_norm, axis=-1, keepdims=True)
    )
    back_state = jnp.einsum(
        "hti,htj->hij", query_heads * head_decay, grad_attended, precision=HIGHEST
    )
    later_state = entering(decay_total, back_state, "seq", True)
    grad_scores = decay_mask * jnp.einsum(
        "htj,hsj->hts", grad_attended, value_heads, precision=HIGHEST
    )
    grad_qh = jnp.einsum(
        "hts,hsi->hti", grad_scores, key_heads, precision=HIGHEST
    ) + head_decay * jnp.einsum("htj,hij->hti", grad_attended, incoming, precision=HIGHEST)
    grad_kh = jnp.einsum(
        "hts,hti->hsi", grad_scores, query_heads, precision=HIGHEST
    ) + tail_decay * jnp.einsum("hsj,hij->hsi", value_heads, later_state, precision=HIGHEST)
    grad_vh = jnp.einsum(
        "hts,htj->hsj", scores, grad_attended, precision=HIGHEST
    ) + tail_decay * jnp.einsum("hsi,hij->hsj", key_heads, later_state, precision=HIGHEST)
    grad_pre = jnp.stack(
        [feature_scale * join_heads(grad_qh), join_heads(grad_kh), join_heads(grad_vh)]
    )
    next_rows = shifted(grad_pre[:, : kernel - 1, :], "seq", -1)
    extended = jnp.concatenate([grad_pre, next_rows], axis=1)
    grad_inputs = jnp.zeros((3, row_count, feat_width), jnp.float32)
    for tap_step in range(kernel):
        grad_inputs = (
            grad_inputs
            + conv_taps[:, tap_step, None, :] * extended[:, tap_step : tap_step + row_count, :]
        )
    tap_terms = jnp.stack(
        [
            jnp.sum(
                grad_pre * padded[:, kernel - 1 - tap_step : kernel - 1 - tap_step + row_count, :],
                axis=1,
            )
            for tap_step in range(kernel)
        ],
        axis=1,
    )
    grad_layout = (grad_pre[0] + grad_pre[1]).astype(jnp.bfloat16)
    table_terms = jnp.stack(
        [
            lax.dot_general(hot_x, grad_layout, contract_first, preferred_element_type=jnp.float32),
            lax.dot_general(hot_y, grad_layout, contract_first, preferred_element_type=jnp.float32),
        ]
    )
    table_rows = 2 * buckets
    tap_rows = 3 * kernel
    packed = jnp.concatenate(
        [
            table_terms.reshape(table_rows, feat_width),
            tap_terms.reshape(tap_rows, feat_width),
            gain_terms.reshape(1, feat_width),
        ]
    )
    summed = lax.psum(packed.astype(jnp.bfloat16), "seq").astype(jnp.float32)
    grad_tables = summed[:table_rows].reshape(2, buckets, feat_width)
    grad_taps = summed[table_rows : table_rows + tap_rows].reshape(3, kernel, feat_width)
    grad_gain = summed[table_rows + tap_rows]
    grad_query = grad_inputs[0].astype(jnp.bfloat16)
    grad_key = grad_inputs[1].astype(jnp.bfloat16)
    grad_value = grad_inputs[2].astype(jnp.bfloat16)
    return (
        layer_out,
        grad_query,
        grad_key,
        grad_value,
        grad_taps,
        grad_tables,
        grad_gain,
        grad_weight,
    )


def solution(mesh):
    return jax.shard_map(
        on_device,
        mesh=mesh,
        in_specs=(
            P("seq", "tp"),
            P("seq", "tp"),
            P("seq", "tp"),
            P(None, None, "tp"),
            P(None, "seq"),
            P(None, None, "tp"),
            P("tp", "seq"),
            P("tp"),
            P("tp", "seq"),
            P("seq", "tp"),
        ),
        out_specs=(
            P("seq", "tp"),
            P("seq", "tp"),
            P("seq", "tp"),
            P("seq", "tp"),
            P(None, None, "tp"),
            P(None, None, "tp"),
            P("tp"),
            P("tp", "seq"),
        ),
        check_vma=False,
    )
```

```python
import jax
import jax.numpy as jnp
from jax import lax
from jax.sharding import PartitionSpec as P

HIGHEST = lax.Precision.HIGHEST


def shifted(x, axis, by):
    length = lax.axis_size(axis)
    pairs = [(i, i + by) for i in range(length) if 0 <= i + by < length]
    return lax.ppermute(x, axis, pairs)


def entering(log_total, state, axis, reverse):
    length = lax.axis_size(axis)
    step = -1 if reverse else 1
    heads, rows, cols = state.shape
    total_rows = jnp.broadcast_to(log_total[:, None, None], (heads, 8, cols))
    packed = shifted(jnp.concatenate([state, total_rows], axis=1), axis, step)
    distance = 1
    while distance < length:
        far = shifted(packed, axis, step * distance)
        near_total = packed[:, rows : rows + 1, :]
        packed = jnp.concatenate(
            [
                jnp.exp(near_total) * far[:, :rows, :] + packed[:, :rows, :],
                far[:, rows:, :] + packed[:, rows:, :],
            ],
            axis=1,
        )
        distance *= 2
    return packed[:, :rows, :]


def on_device(
    query_raw,
    key_raw,
    value_raw,
    conv_taps,
    layout_boxes,
    box_tables,
    log_decay,
    norm_gain,
    out_weight,
    grad_output,
):
    row_count, feat_width = query_raw.shape
    head_count = log_decay.shape[0]
    head_size = feat_width // head_count
    kernel = conv_taps.shape[1]
    buckets = box_tables.shape[1]
    feature_scale = head_size ** (-0.5)
    stacked = jnp.stack([query_raw, key_raw, value_raw])
    rim_rows = shifted(stacked[:, row_count - (kernel - 1) :, :], "seq", 1)
    padded = jnp.concatenate([rim_rows, stacked], axis=1).astype(jnp.float32)
    conved = jnp.zeros((3, row_count, feat_width), jnp.float32)
    for tap_step in range(kernel):
        conved = (
            conved
            + conv_taps[:, tap_step, None, :]
            * padded[:, kernel - 1 - tap_step : kernel - 1 - tap_step + row_count, :]
        )
    bucket_ids = jnp.arange(buckets, dtype=jnp.int32)

    def count_table(first, second):
        return (first[:, None] == bucket_ids[None, :]).astype(jnp.bfloat16) + (
            second[:, None] == bucket_ids[None, :]
        ).astype(jnp.bfloat16)

    hot_x = count_table(layout_boxes[0], layout_boxes[2])
    hot_y = count_table(layout_boxes[1], layout_boxes[3])
    layout = jnp.dot(hot_x, box_tables[0], preferred_element_type=jnp.float32) + jnp.dot(
        hot_y, box_tables[1], preferred_element_type=jnp.float32
    )
    query_feat = (feature_scale * (conved[0] + layout)).astype(jnp.bfloat16)
    key_feat = (conved[1] + layout).astype(jnp.bfloat16)
    value_feat = conved[2].astype(jnp.bfloat16)

    def split_heads(matrix):
        return matrix.reshape(row_count, head_count, head_size).transpose(1, 0, 2)

    def join_heads(blocks):
        return blocks.transpose(1, 0, 2).reshape(row_count, feat_width)

    query_heads = split_heads(query_feat)
    key_heads = split_heads(key_feat)
    value_heads = split_heads(value_feat)
    decay_sum = jnp.cumsum(log_decay, axis=1)
    decay_total = decay_sum[:, -1]
    head_decay = jnp.exp(decay_sum)[:, :, None]
    tail_decay = jnp.exp(decay_total[:, None] - decay_sum)[:, :, None]
    positions = jnp.arange(row_count, dtype=jnp.int32)
    causal_mask = positions[:, None] >= positions[None, :]
    decay_mask = jnp.where(
        causal_mask[None],
        jnp.exp(jnp.minimum(decay_sum[:, :, None] - decay_sum[:, None, :], 0.0)),
        0.0,
    )
    local_state = jnp.einsum("hsi,hsj->hij", key_heads * tail_decay, value_heads, precision=HIGHEST)
    incoming = entering(decay_total, local_state, "seq", False)
    scores = decay_mask * jnp.einsum(
        "hti,hsi->hts", query_heads, key_heads, preferred_element_type=jnp.float32
    )
    attended = jnp.einsum("hts,hsj->htj", scores, value_heads, precision=HIGHEST)
    attended = attended + head_decay * jnp.einsum(
        "hti,hij->htj", query_heads, incoming, precision=HIGHEST
    )
    inverse = lax.rsqrt(jnp.mean(attended * attended, axis=-1, keepdims=True) + 1e-06)
    unit_norm = attended * inverse
    gain_heads = norm_gain.reshape(head_count, 1, head_size)
    normed = join_heads(unit_norm * gain_heads).astype(jnp.bfloat16)
    partial_sum = jnp.dot(
        normed,
        lax.all_gather(out_weight, "seq", axis=1, tiled=True),
        preferred_element_type=jnp.float32,
    )
    layer_out = lax.psum_scatter(
        partial_sum.astype(jnp.bfloat16), "tp", scatter_dimension=1, tiled=True
    )
    cotangent = lax.all_gather(grad_output, "tp", axis=1, tiled=True)
    contract_last = (((1,), (1,)), ((), ()))
    grad_normed_sum = lax.dot_general(
        cotangent,
        lax.all_gather(out_weight, "seq", axis=1, tiled=True),
        contract_last,
        preferred_element_type=jnp.float32,
    )
    grad_normed = grad_normed_sum.astype(jnp.bfloat16)
    contract_first = (((0,), (0,)), ((), ()))
    weight_terms = lax.dot_general(
        normed, cotangent, contract_first, preferred_element_type=jnp.float32
    )
    seq_count = lax.axis_size("seq")
    col_block = weight_terms.shape[1] // seq_count
    weight_parts = (
        weight_terms.astype(jnp.bfloat16)
        .reshape(feat_width, seq_count, col_block)
        .transpose(1, 0, 2)
    )
    weight_parts = lax.all_to_all(weight_parts, "seq", 0, 0, tiled=True)
    grad_weight = jnp.sum(weight_parts.astype(jnp.float32), axis=0)
    grad_heads = split_heads(grad_normed).astype(jnp.float32)
    gain_terms = jnp.sum(grad_heads * unit_norm, axis=1).reshape(feat_width)
    grad_unit = grad_heads * gain_heads
    grad_attended = inverse * (
        grad_unit - unit_norm * jnp.mean(grad_unit * unit_norm, axis=-1, keepdims=True)
    )
    back_state = jnp.einsum(
        "hti,htj->hij", query_heads * head_decay, grad_attended, precision=HIGHEST
    )
    later_state = entering(decay_total, back_state, "seq", True)
    grad_scores = decay_mask * jnp.einsum(
        "htj,hsj->hts", grad_attended, value_heads, precision=HIGHEST
    )
    grad_qh = jnp.einsum(
        "hts,hsi->hti", grad_scores, key_heads, precision=HIGHEST
    ) + head_decay * jnp.einsum("htj,hij->hti", grad_attended, incoming, precision=HIGHEST)
    grad_kh = jnp.einsum(
        "hts,hti->hsi", grad_scores, query_heads, precision=HIGHEST
    ) + tail_decay * jnp.einsum("hsj,hij->hsi", value_heads, later_state, precision=HIGHEST)
    grad_vh = jnp.einsum(
        "hts,htj->hsj", scores, grad_attended, precision=HIGHEST
    ) + tail_decay * jnp.einsum("hsi,hij->hsj", key_heads, later_state, precision=HIGHEST)
    grad_pre = jnp.stack(
        [feature_scale * join_heads(grad_qh), join_heads(grad_kh), join_heads(grad_vh)]
    )
    next_rows = shifted(grad_pre[:, : kernel - 1, :], "seq", -1)
    extended = jnp.concatenate([grad_pre, next_rows], axis=1)
    grad_inputs = jnp.zeros((3, row_count, feat_width), jnp.float32)
    for tap_step in range(kernel):
        grad_inputs = (
            grad_inputs
            + conv_taps[:, tap_step, None, :] * extended[:, tap_step : tap_step + row_count, :]
        )
    tap_terms = jnp.stack(
        [
            jnp.sum(
                grad_pre * padded[:, kernel - 1 - tap_step : kernel - 1 - tap_step + row_count, :],
                axis=1,
            )
            for tap_step in range(kernel)
        ],
        axis=1,
    )
    grad_layout = (grad_pre[0] + grad_pre[1]).astype(jnp.bfloat16)
    table_terms = jnp.stack(
        [
            lax.dot_general(hot_x, grad_layout, contract_first, preferred_element_type=jnp.float32),
            lax.dot_general(hot_y, grad_layout, contract_first, preferred_element_type=jnp.float32),
        ]
    )
    table_rows = 2 * buckets
    tap_rows = 3 * kernel
    packed = jnp.concatenate(
        [
            table_terms.reshape(table_rows, feat_width),
            tap_terms.reshape(tap_rows, feat_width),
            gain_terms.reshape(1, feat_width),
        ]
    )
    packed, layer_out = lax.optimization_barrier((packed, layer_out))
    summed = lax.psum(packed.astype(jnp.bfloat16), "seq").astype(jnp.float32)
    grad_tables = summed[:table_rows].reshape(2, buckets, feat_width)
    grad_taps = summed[table_rows : table_rows + tap_rows].reshape(3, kernel, feat_width)
    grad_gain = summed[table_rows + tap_rows]
    grad_query = grad_inputs[0].astype(jnp.bfloat16)
    grad_key = grad_inputs[1].astype(jnp.bfloat16)
    grad_value = grad_inputs[2].astype(jnp.bfloat16)
    return (
        layer_out,
        grad_query,
        grad_key,
        grad_value,
        grad_taps,
        grad_tables,
        grad_gain,
        grad_weight,
    )


def solution(mesh):
    return jax.shard_map(
        on_device,
        mesh=mesh,
        in_specs=(
            P("seq", "tp"),
            P("seq", "tp"),
            P("seq", "tp"),
            P(None, None, "tp"),
            P(None, "seq"),
            P(None, None, "tp"),
            P("tp", "seq"),
            P("tp"),
            P("tp", "seq"),
            P("seq", "tp"),
        ),
        out_specs=(
            P("seq", "tp"),
            P("seq", "tp"),
            P("seq", "tp"),
            P("seq", "tp"),
            P(None, None, "tp"),
            P(None, None, "tp"),
            P("tp"),
            P("tp", "seq"),
        ),
        check_vma=False,
    )
```

```python
import jax
import jax.numpy as jnp
from jax import lax
from jax.sharding import PartitionSpec as P

HIGHEST = lax.Precision.HIGHEST


def shifted(x, axis, by):
    length = lax.axis_size(axis)
    pairs = [(i, i + by) for i in range(length) if 0 <= i + by < length]
    return lax.ppermute(x, axis, pairs)


def entering(log_total, state, axis, reverse):
    length = lax.axis_size(axis)
    step = -1 if reverse else 1
    heads, rows, cols = state.shape
    total_rows = jnp.broadcast_to(log_total[:, None, None], (heads, 8, cols))
    packed = shifted(jnp.concatenate([state, total_rows], axis=1), axis, step)
    distance = 1
    while distance < length:
        far = shifted(packed, axis, step * distance)
        near_total = packed[:, rows : rows + 1, :]
        packed = jnp.concatenate(
            [
                jnp.exp(near_total) * far[:, :rows, :] + packed[:, :rows, :],
                far[:, rows:, :] + packed[:, rows:, :],
            ],
            axis=1,
        )
        distance *= 2
    return packed[:, :rows, :]


def on_device(
    query_raw,
    key_raw,
    value_raw,
    conv_taps,
    layout_boxes,
    box_tables,
    log_decay,
    norm_gain,
    out_weight,
    grad_output,
):
    row_count, feat_width = query_raw.shape
    head_count = log_decay.shape[0]
    head_size = feat_width // head_count
    kernel = conv_taps.shape[1]
    buckets = box_tables.shape[1]
    feature_scale = head_size ** (-0.5)
    stacked = jnp.stack([query_raw, key_raw, value_raw])
    rim_rows = shifted(stacked[:, row_count - (kernel - 1) :, :], "seq", 1)
    padded = jnp.concatenate([rim_rows, stacked], axis=1).astype(jnp.float32)
    conved = jnp.zeros((3, row_count, feat_width), jnp.float32)
    for tap_step in range(kernel):
        conved = (
            conved
            + conv_taps[:, tap_step, None, :]
            * padded[:, kernel - 1 - tap_step : kernel - 1 - tap_step + row_count, :]
        )
    bucket_ids = jnp.arange(buckets, dtype=jnp.int32)

    def count_table(first, second):
        return (first[:, None] == bucket_ids[None, :]).astype(jnp.bfloat16) + (
            second[:, None] == bucket_ids[None, :]
        ).astype(jnp.bfloat16)

    hot_x = count_table(layout_boxes[0], layout_boxes[2])
    hot_y = count_table(layout_boxes[1], layout_boxes[3])
    layout = jnp.dot(hot_x, box_tables[0], preferred_element_type=jnp.float32) + jnp.dot(
        hot_y, box_tables[1], preferred_element_type=jnp.float32
    )
    query_feat = (feature_scale * (conved[0] + layout)).astype(jnp.bfloat16)
    key_feat = (conved[1] + layout).astype(jnp.bfloat16)
    value_feat = conved[2].astype(jnp.bfloat16)

    def split_heads(matrix):
        return matrix.reshape(row_count, head_count, head_size).transpose(1, 0, 2)

    def join_heads(blocks):
        return blocks.transpose(1, 0, 2).reshape(row_count, feat_width)

    query_heads = split_heads(query_feat)
    key_heads = split_heads(key_feat)
    value_heads = split_heads(value_feat)
    decay_sum = jnp.cumsum(log_decay, axis=1)
    decay_total = decay_sum[:, -1]
    head_decay = jnp.exp(decay_sum)[:, :, None]
    tail_decay = jnp.exp(decay_total[:, None] - decay_sum)[:, :, None]
    positions = jnp.arange(row_count, dtype=jnp.int32)
    causal_mask = positions[:, None] >= positions[None, :]
    decay_mask = jnp.where(
        causal_mask[None],
        jnp.exp(jnp.minimum(decay_sum[:, :, None] - decay_sum[:, None, :], 0.0)),
        0.0,
    )
    local_state = jnp.einsum("hsi,hsj->hij", key_heads * tail_decay, value_heads, precision=HIGHEST)
    incoming = entering(decay_total, local_state, "seq", False)
    scores = decay_mask * jnp.einsum(
        "hti,hsi->hts", query_heads, key_heads, preferred_element_type=jnp.float32
    )
    attended = jnp.einsum("hts,hsj->htj", scores, value_heads, precision=HIGHEST)
    attended = attended + head_decay * jnp.einsum(
        "hti,hij->htj", query_heads, incoming, precision=HIGHEST
    )
    inverse = lax.rsqrt(jnp.mean(attended * attended, axis=-1, keepdims=True) + 1e-06)
    unit_norm = attended * inverse
    gain_heads = norm_gain.reshape(head_count, 1, head_size)
    normed = join_heads(unit_norm * gain_heads).astype(jnp.bfloat16)
    partial_sum = jnp.dot(
        normed,
        lax.all_gather(out_weight, "seq", axis=1, tiled=True),
        preferred_element_type=jnp.float32,
    )
    layer_out = lax.psum_scatter(
        partial_sum.astype(jnp.bfloat16), "tp", scatter_dimension=1, tiled=True
    )
    cotangent = lax.all_gather(grad_output, "tp", axis=1, tiled=True)
    contract_last = (((1,), (1,)), ((), ()))
    grad_normed_sum = lax.dot_general(
        cotangent,
        lax.all_gather(out_weight, "seq", axis=1, tiled=True),
        contract_last,
        preferred_element_type=jnp.float32,
    )
    grad_normed = grad_normed_sum.astype(jnp.bfloat16)
    contract_first = (((0,), (0,)), ((), ()))
    weight_terms = lax.dot_general(
        normed, cotangent, contract_first, preferred_element_type=jnp.float32
    )
    grad_heads = split_heads(grad_normed).astype(jnp.float32)
    gain_terms = jnp.sum(grad_heads * unit_norm, axis=1).reshape(feat_width)
    grad_unit = grad_heads * gain_heads
    grad_attended = inverse * (
        grad_unit - unit_norm * jnp.mean(grad_unit * unit_norm, axis=-1, keepdims=True)
    )
    back_state = jnp.einsum(
        "hti,htj->hij", query_heads * head_decay, grad_attended, precision=HIGHEST
    )
    later_state = entering(decay_total, back_state, "seq", True)
    seq_count = lax.axis_size("seq")
    col_block = weight_terms.shape[1] // seq_count
    weight_parts = (
        weight_terms.astype(jnp.bfloat16)
        .reshape(feat_width, seq_count, col_block)
        .transpose(1, 0, 2)
    )
    weight_parts, later_state = lax.optimization_barrier((weight_parts, later_state))
    weight_parts = lax.all_to_all(weight_parts, "seq", 0, 0, tiled=True)
    grad_weight = jnp.sum(weight_parts.astype(jnp.float32), axis=0)
    grad_scores = decay_mask * jnp.einsum(
        "htj,hsj->hts", grad_attended, value_heads, precision=HIGHEST
    )
    grad_qh = jnp.einsum(
        "hts,hsi->hti", grad_scores, key_heads, precision=HIGHEST
    ) + head_decay * jnp.einsum("htj,hij->hti", grad_attended, incoming, precision=HIGHEST)
    grad_kh = jnp.einsum(
        "hts,hti->hsi", grad_scores, query_heads, precision=HIGHEST
    ) + tail_decay * jnp.einsum("hsj,hij->hsi", value_heads, later_state, precision=HIGHEST)
    grad_vh = jnp.einsum(
        "hts,htj->hsj", scores, grad_attended, precision=HIGHEST
    ) + tail_decay * jnp.einsum("hsi,hij->hsj", key_heads, later_state, precision=HIGHEST)
    grad_pre = jnp.stack(
        [feature_scale * join_heads(grad_qh), join_heads(grad_kh), join_heads(grad_vh)]
    )
    next_rows = shifted(grad_pre[:, : kernel - 1, :], "seq", -1)
    extended = jnp.concatenate([grad_pre, next_rows], axis=1)
    grad_inputs = jnp.zeros((3, row_count, feat_width), jnp.float32)
    for tap_step in range(kernel):
        grad_inputs = (
            grad_inputs
            + conv_taps[:, tap_step, None, :] * extended[:, tap_step : tap_step + row_count, :]
        )
    tap_terms = jnp.stack(
        [
            jnp.sum(
                grad_pre * padded[:, kernel - 1 - tap_step : kernel - 1 - tap_step + row_count, :],
                axis=1,
            )
            for tap_step in range(kernel)
        ],
        axis=1,
    )
    grad_layout = (grad_pre[0] + grad_pre[1]).astype(jnp.bfloat16)
    table_terms = jnp.stack(
        [
            lax.dot_general(hot_x, grad_layout, contract_first, preferred_element_type=jnp.float32),
            lax.dot_general(hot_y, grad_layout, contract_first, preferred_element_type=jnp.float32),
        ]
    )
    table_rows = 2 * buckets
    tap_rows = 3 * kernel
    packed = jnp.concatenate(
        [
            table_terms.reshape(table_rows, feat_width),
            tap_terms.reshape(tap_rows, feat_width),
            gain_terms.reshape(1, feat_width),
        ]
    )
    packed, layer_out = lax.optimization_barrier((packed, layer_out))
    summed = lax.psum(packed.astype(jnp.bfloat16), "seq").astype(jnp.float32)
    grad_tables = summed[:table_rows].reshape(2, buckets, feat_width)
    grad_taps = summed[table_rows : table_rows + tap_rows].reshape(3, kernel, feat_width)
    grad_gain = summed[table_rows + tap_rows]
    grad_query = grad_inputs[0].astype(jnp.bfloat16)
    grad_key = grad_inputs[1].astype(jnp.bfloat16)
    grad_value = grad_inputs[2].astype(jnp.bfloat16)
    return (
        layer_out,
        grad_query,
        grad_key,
        grad_value,
        grad_taps,
        grad_tables,
        grad_gain,
        grad_weight,
    )


def solution(mesh):
    return jax.shard_map(
        on_device,
        mesh=mesh,
        in_specs=(
            P("seq", "tp"),
            P("seq", "tp"),
            P("seq", "tp"),
            P(None, None, "tp"),
            P(None, "seq"),
            P(None, None, "tp"),
            P("tp", "seq"),
            P("tp"),
            P("tp", "seq"),
            P("seq", "tp"),
        ),
        out_specs=(
            P("seq", "tp"),
            P("seq", "tp"),
            P("seq", "tp"),
            P("seq", "tp"),
            P(None, None, "tp"),
            P(None, None, "tp"),
            P("tp"),
            P("tp", "seq"),
        ),
        check_vma=False,
    )
```

```python
import jax
import jax.numpy as jnp
from jax import lax
from jax.sharding import PartitionSpec as P

HIGHEST = lax.Precision.HIGHEST


def shifted(x, axis, by):
    length = lax.axis_size(axis)
    pairs = [(i, i + by) for i in range(length) if 0 <= i + by < length]
    return lax.ppermute(x, axis, pairs)


def entering(log_total, state, axis, reverse):
    length = lax.axis_size(axis)
    step = -1 if reverse else 1
    heads, rows, cols = state.shape
    total_rows = jnp.broadcast_to(log_total[:, None, None], (heads, 8, cols))
    packed = shifted(jnp.concatenate([state, total_rows], axis=1), axis, step)
    distance = 1
    while distance < length:
        far = shifted(packed, axis, step * distance)
        near_total = packed[:, rows : rows + 1, :]
        packed = jnp.concatenate(
            [
                jnp.exp(near_total) * far[:, :rows, :] + packed[:, :rows, :],
                far[:, rows:, :] + packed[:, rows:, :],
            ],
            axis=1,
        )
        distance *= 2
    return packed[:, :rows, :]


def on_device(
    query_raw,
    key_raw,
    value_raw,
    conv_taps,
    layout_boxes,
    box_tables,
    log_decay,
    norm_gain,
    out_weight,
    grad_output,
):
    row_count, feat_width = query_raw.shape
    head_count = log_decay.shape[0]
    head_size = feat_width // head_count
    kernel = conv_taps.shape[1]
    buckets = box_tables.shape[1]
    feature_scale = head_size ** (-0.5)
    stacked = jnp.stack([query_raw, key_raw, value_raw])
    rim_rows = shifted(stacked[:, row_count - (kernel - 1) :, :], "seq", 1)
    padded = jnp.concatenate([rim_rows, stacked], axis=1).astype(jnp.float32)
    conved = jnp.zeros((3, row_count, feat_width), jnp.float32)
    for tap_step in range(kernel):
        conved = (
            conved
            + conv_taps[:, tap_step, None, :]
            * padded[:, kernel - 1 - tap_step : kernel - 1 - tap_step + row_count, :]
        )
    bucket_ids = jnp.arange(buckets, dtype=jnp.int32)

    def count_table(first, second):
        return (first[:, None] == bucket_ids[None, :]).astype(jnp.bfloat16) + (
            second[:, None] == bucket_ids[None, :]
        ).astype(jnp.bfloat16)

    hot_x = count_table(layout_boxes[0], layout_boxes[2])
    hot_y = count_table(layout_boxes[1], layout_boxes[3])
    layout = jnp.dot(hot_x, box_tables[0], preferred_element_type=jnp.float32) + jnp.dot(
        hot_y, box_tables[1], preferred_element_type=jnp.float32
    )
    query_feat = (feature_scale * (conved[0] + layout)).astype(jnp.bfloat16)
    key_feat = (conved[1] + layout).astype(jnp.bfloat16)
    value_feat = conved[2].astype(jnp.bfloat16)

    def split_heads(matrix):
        return matrix.reshape(row_count, head_count, head_size).transpose(1, 0, 2)

    def join_heads(blocks):
        return blocks.transpose(1, 0, 2).reshape(row_count, feat_width)

    query_heads = split_heads(query_feat)
    key_heads = split_heads(key_feat)
    value_heads = split_heads(value_feat)
    decay_sum = jnp.cumsum(log_decay, axis=1)
    decay_total = decay_sum[:, -1]
    head_decay = jnp.exp(decay_sum)[:, :, None]
    tail_decay = jnp.exp(decay_total[:, None] - decay_sum)[:, :, None]
    positions = jnp.arange(row_count, dtype=jnp.int32)
    causal_mask = positions[:, None] >= positions[None, :]
    decay_mask = jnp.where(
        causal_mask[None],
        jnp.exp(jnp.minimum(decay_sum[:, :, None] - decay_sum[:, None, :], 0.0)),
        0.0,
    )
    local_state = jnp.einsum("hsi,hsj->hij", key_heads * tail_decay, value_heads, precision=HIGHEST)
    incoming = entering(decay_total, local_state, "seq", False)
    scores = decay_mask * jnp.einsum(
        "hti,hsi->hts", query_heads, key_heads, preferred_element_type=jnp.float32
    )
    attended = jnp.einsum("hts,hsj->htj", scores, value_heads, precision=HIGHEST)
    attended = attended + head_decay * jnp.einsum(
        "hti,hij->htj", query_heads, incoming, precision=HIGHEST
    )
    inverse = lax.rsqrt(jnp.mean(attended * attended, axis=-1, keepdims=True) + 1e-06)
    unit_norm = attended * inverse
    gain_heads = norm_gain.reshape(head_count, 1, head_size)
    normed = join_heads(unit_norm * gain_heads).astype(jnp.bfloat16)
    partial_sum = jnp.dot(
        normed,
        lax.all_gather(out_weight, "seq", axis=1, tiled=True),
        preferred_element_type=jnp.float32,
    )
    layer_out = lax.psum_scatter(
        partial_sum.astype(jnp.bfloat16), "tp", scatter_dimension=1, tiled=True
    )
    cotangent = lax.all_gather(grad_output, "tp", axis=1, tiled=True)
    contract_last = (((1,), (1,)), ((), ()))
    grad_normed_sum = lax.dot_general(
        cotangent,
        lax.all_gather(out_weight, "seq", axis=1, tiled=True),
        contract_last,
        preferred_element_type=jnp.float32,
    )
    grad_normed = grad_normed_sum.astype(jnp.bfloat16)
    contract_first = (((0,), (0,)), ((), ()))
    weight_terms = lax.dot_general(
        normed, cotangent, contract_first, preferred_element_type=jnp.float32
    )
    grad_heads = split_heads(grad_normed).astype(jnp.float32)
    gain_terms = jnp.sum(grad_heads * unit_norm, axis=1).reshape(feat_width)
    grad_unit = grad_heads * gain_heads
    grad_attended = inverse * (
        grad_unit - unit_norm * jnp.mean(grad_unit * unit_norm, axis=-1, keepdims=True)
    )
    back_state = jnp.einsum(
        "hti,htj->hij", query_heads * head_decay, grad_attended, precision=HIGHEST
    )
    later_state = entering(decay_total, back_state, "seq", True)
    seq_count = lax.axis_size("seq")
    col_block = weight_terms.shape[1] // seq_count
    weight_parts = (
        weight_terms.astype(jnp.bfloat16)
        .reshape(feat_width, seq_count, col_block)
        .transpose(1, 0, 2)
    )
    weight_parts, later_state = lax.optimization_barrier((weight_parts, later_state))
    grad_scores = decay_mask * jnp.einsum(
        "htj,hsj->hts", grad_attended, value_heads, precision=HIGHEST
    )
    grad_qh = jnp.einsum(
        "hts,hsi->hti", grad_scores, key_heads, precision=HIGHEST
    ) + head_decay * jnp.einsum("htj,hij->hti", grad_attended, incoming, precision=HIGHEST)
    grad_kh = jnp.einsum(
        "hts,hti->hsi", grad_scores, query_heads, precision=HIGHEST
    ) + tail_decay * jnp.einsum("hsj,hij->hsi", value_heads, later_state, precision=HIGHEST)
    grad_vh = jnp.einsum(
        "hts,htj->hsj", scores, grad_attended, precision=HIGHEST
    ) + tail_decay * jnp.einsum("hsi,hij->hsj", key_heads, later_state, precision=HIGHEST)
    grad_pre = jnp.stack(
        [feature_scale * join_heads(grad_qh), join_heads(grad_kh), join_heads(grad_vh)]
    )
    next_rows = shifted(grad_pre[:, : kernel - 1, :], "seq", -1)
    extended = jnp.concatenate([grad_pre, next_rows], axis=1)
    grad_inputs = jnp.zeros((3, row_count, feat_width), jnp.float32)
    for tap_step in range(kernel):
        grad_inputs = (
            grad_inputs
            + conv_taps[:, tap_step, None, :] * extended[:, tap_step : tap_step + row_count, :]
        )
    tap_terms = jnp.stack(
        [
            jnp.sum(
                grad_pre * padded[:, kernel - 1 - tap_step : kernel - 1 - tap_step + row_count, :],
                axis=1,
            )
            for tap_step in range(kernel)
        ],
        axis=1,
    )
    grad_layout = (grad_pre[0] + grad_pre[1]).astype(jnp.bfloat16)
    table_terms = jnp.stack(
        [
            lax.dot_general(hot_x, grad_layout, contract_first, preferred_element_type=jnp.float32),
            lax.dot_general(hot_y, grad_layout, contract_first, preferred_element_type=jnp.float32),
        ]
    )
    table_rows = 2 * buckets
    tap_rows = 3 * kernel
    packed = jnp.concatenate(
        [
            table_terms.astype(jnp.bfloat16).reshape(table_rows, feat_width),
            tap_terms.astype(jnp.bfloat16).reshape(tap_rows, feat_width),
            gain_terms.astype(jnp.bfloat16).reshape(1, feat_width),
        ]
    )
    packed, layer_out, weight_parts = lax.optimization_barrier((packed, layer_out, weight_parts))
    summed = lax.psum(packed, "seq").astype(jnp.float32)
    weight_parts = lax.all_to_all(weight_parts, "seq", 0, 0, tiled=True)
    grad_weight = jnp.sum(weight_parts.astype(jnp.float32), axis=0)
    grad_tables = summed[:table_rows].reshape(2, buckets, feat_width)
    grad_taps = summed[table_rows : table_rows + tap_rows].reshape(3, kernel, feat_width)
    grad_gain = summed[table_rows + tap_rows]
    grad_query = grad_inputs[0].astype(jnp.bfloat16)
    grad_key = grad_inputs[1].astype(jnp.bfloat16)
    grad_value = grad_inputs[2].astype(jnp.bfloat16)
    return (
        layer_out,
        grad_query,
        grad_key,
        grad_value,
        grad_taps,
        grad_tables,
        grad_gain,
        grad_weight,
    )


def solution(mesh):
    return jax.shard_map(
        on_device,
        mesh=mesh,
        in_specs=(
            P("seq", "tp"),
            P("seq", "tp"),
            P("seq", "tp"),
            P(None, None, "tp"),
            P(None, "seq"),
            P(None, None, "tp"),
            P("tp", "seq"),
            P("tp"),
            P("tp", "seq"),
            P("seq", "tp"),
        ),
        out_specs=(
            P("seq", "tp"),
            P("seq", "tp"),
            P("seq", "tp"),
            P("seq", "tp"),
            P(None, None, "tp"),
            P(None, None, "tp"),
            P("tp"),
            P("tp", "seq"),
        ),
        check_vma=False,
    )
```

```python
import jax
import jax.numpy as jnp
from jax import lax
from jax.sharding import PartitionSpec as P

HIGHEST = lax.Precision.HIGHEST


def shifted(x, axis, by):
    length = lax.axis_size(axis)
    pairs = [(i, i + by) for i in range(length) if 0 <= i + by < length]
    return lax.ppermute(x, axis, pairs)


def exchanged(log_total, state, axis, by):
    heads, rows, cols = state.shape
    high = log_total.astype(jnp.bfloat16)
    low = (log_total - high.astype(jnp.float32)).astype(jnp.bfloat16)
    message = jnp.concatenate(
        [
            state.astype(jnp.bfloat16),
            jnp.broadcast_to(high[:, None, None], (heads, 8, cols)),
            jnp.broadcast_to(low[:, None, None], (heads, 8, cols)),
        ],
        axis=1,
    )
    message = shifted(message, axis, by).astype(jnp.float32)
    return message[:, rows, 0] + message[:, rows + 8, 0], message[:, :rows, :]


def entering(log_total, state, axis, reverse):
    length = lax.axis_size(axis)
    step = -1 if reverse else 1
    log_total, state = exchanged(log_total, state, axis, step)
    distance = 1
    while distance < length:
        far_total, far_state = exchanged(log_total, state, axis, step * distance)
        state = jnp.exp(log_total)[:, None, None] * far_state + state
        log_total = far_total + log_total
        distance *= 2
    return state


def on_device(
    query_raw,
    key_raw,
    value_raw,
    conv_taps,
    layout_boxes,
    box_tables,
    log_decay,
    norm_gain,
    out_weight,
    grad_output,
):
    row_count, feat_width = query_raw.shape
    head_count = log_decay.shape[0]
    head_size = feat_width // head_count
    kernel = conv_taps.shape[1]
    buckets = box_tables.shape[1]
    feature_scale = head_size ** (-0.5)
    stacked = jnp.stack([query_raw, key_raw, value_raw])
    rim_rows = shifted(stacked[:, row_count - (kernel - 1) :, :], "seq", 1)
    padded = jnp.concatenate([rim_rows, stacked], axis=1).astype(jnp.float32)
    conved = jnp.zeros((3, row_count, feat_width), jnp.float32)
    for tap_step in range(kernel):
        conved = (
            conved
            + conv_taps[:, tap_step, None, :]
            * padded[:, kernel - 1 - tap_step : kernel - 1 - tap_step + row_count, :]
        )
    bucket_ids = jnp.arange(buckets, dtype=jnp.int32)

    def count_table(first, second):
        return (first[:, None] == bucket_ids[None, :]).astype(jnp.bfloat16) + (
            second[:, None] == bucket_ids[None, :]
        ).astype(jnp.bfloat16)

    hot_x = count_table(layout_boxes[0], layout_boxes[2])
    hot_y = count_table(layout_boxes[1], layout_boxes[3])
    layout = jnp.dot(hot_x, box_tables[0], preferred_element_type=jnp.float32) + jnp.dot(
        hot_y, box_tables[1], preferred_element_type=jnp.float32
    )
    query_feat = (feature_scale * (conved[0] + layout)).astype(jnp.bfloat16)
    key_feat = (conved[1] + layout).astype(jnp.bfloat16)
    value_feat = conved[2].astype(jnp.bfloat16)

    def split_heads(matrix):
        return matrix.reshape(row_count, head_count, head_size).transpose(1, 0, 2)

    def join_heads(blocks):
        return blocks.transpose(1, 0, 2).reshape(row_count, feat_width)

    query_heads = split_heads(query_feat)
    key_heads = split_heads(key_feat)
    value_heads = split_heads(value_feat)
    decay_sum = jnp.cumsum(log_decay, axis=1)
    decay_total = decay_sum[:, -1]
    head_decay = jnp.exp(decay_sum)[:, :, None]
    tail_decay = jnp.exp(decay_total[:, None] - decay_sum)[:, :, None]
    positions = jnp.arange(row_count, dtype=jnp.int32)
    causal_mask = positions[:, None] >= positions[None, :]
    decay_mask = jnp.where(
        causal_mask[None],
        jnp.exp(jnp.minimum(decay_sum[:, :, None] - decay_sum[:, None, :], 0.0)),
        0.0,
    )
    local_state = jnp.einsum("hsi,hsj->hij", key_heads * tail_decay, value_heads, precision=HIGHEST)
    incoming = entering(decay_total, local_state, "seq", False)
    scores = decay_mask * jnp.einsum(
        "hti,hsi->hts", query_heads, key_heads, preferred_element_type=jnp.float32
    )
    attended = jnp.einsum("hts,hsj->htj", scores, value_heads, precision=HIGHEST)
    attended = attended + head_decay * jnp.einsum(
        "hti,hij->htj", query_heads, incoming, precision=HIGHEST
    )
    inverse = lax.rsqrt(jnp.mean(attended * attended, axis=-1, keepdims=True) + 1e-06)
    unit_norm = attended * inverse
    gain_heads = norm_gain.reshape(head_count, 1, head_size)
    normed = join_heads(unit_norm * gain_heads).astype(jnp.bfloat16)
    partial_sum = jnp.dot(
        normed,
        lax.all_gather(out_weight, "seq", axis=1, tiled=True),
        preferred_element_type=jnp.float32,
    )
    layer_out = lax.psum_scatter(
        partial_sum.astype(jnp.bfloat16), "tp", scatter_dimension=1, tiled=True
    )
    cotangent = lax.all_gather(grad_output, "tp", axis=1, tiled=True)
    contract_last = (((1,), (1,)), ((), ()))
    grad_normed_sum = lax.dot_general(
        cotangent,
        lax.all_gather(out_weight, "seq", axis=1, tiled=True),
        contract_last,
        preferred_element_type=jnp.float32,
    )
    grad_normed = grad_normed_sum.astype(jnp.bfloat16)
    contract_first = (((0,), (0,)), ((), ()))
    weight_terms = lax.dot_general(
        normed, cotangent, contract_first, preferred_element_type=jnp.float32
    )
    grad_heads = split_heads(grad_normed).astype(jnp.float32)
    gain_terms = jnp.sum(grad_heads * unit_norm, axis=1).reshape(feat_width)
    grad_unit = grad_heads * gain_heads
    grad_attended = inverse * (
        grad_unit - unit_norm * jnp.mean(grad_unit * unit_norm, axis=-1, keepdims=True)
    )
    back_state = jnp.einsum(
        "hti,htj->hij", query_heads * head_decay, grad_attended, precision=HIGHEST
    )
    later_state = entering(decay_total, back_state, "seq", True)
    seq_count = lax.axis_size("seq")
    col_block = weight_terms.shape[1] // seq_count
    weight_parts = (
        weight_terms.astype(jnp.bfloat16)
        .reshape(feat_width, seq_count, col_block)
        .transpose(1, 0, 2)
    )
    weight_parts, later_state = lax.optimization_barrier((weight_parts, later_state))
    grad_scores = decay_mask * jnp.einsum(
        "htj,hsj->hts", grad_attended, value_heads, precision=HIGHEST
    )
    grad_qh = jnp.einsum(
        "hts,hsi->hti", grad_scores, key_heads, precision=HIGHEST
    ) + head_decay * jnp.einsum("htj,hij->hti", grad_attended, incoming, precision=HIGHEST)
    grad_kh = jnp.einsum(
        "hts,hti->hsi", grad_scores, query_heads, precision=HIGHEST
    ) + tail_decay * jnp.einsum("hsj,hij->hsi", value_heads, later_state, precision=HIGHEST)
    grad_vh = jnp.einsum(
        "hts,htj->hsj", scores, grad_attended, precision=HIGHEST
    ) + tail_decay * jnp.einsum("hsi,hij->hsj", key_heads, later_state, precision=HIGHEST)
    grad_pre = jnp.stack(
        [feature_scale * join_heads(grad_qh), join_heads(grad_kh), join_heads(grad_vh)]
    )
    next_rows = shifted(grad_pre[:, : kernel - 1, :], "seq", -1)
    extended = jnp.concatenate([grad_pre, next_rows], axis=1)
    grad_inputs = jnp.zeros((3, row_count, feat_width), jnp.float32)
    for tap_step in range(kernel):
        grad_inputs = (
            grad_inputs
            + conv_taps[:, tap_step, None, :] * extended[:, tap_step : tap_step + row_count, :]
        )
    tap_terms = jnp.stack(
        [
            jnp.sum(
                grad_pre * padded[:, kernel - 1 - tap_step : kernel - 1 - tap_step + row_count, :],
                axis=1,
            )
            for tap_step in range(kernel)
        ],
        axis=1,
    )
    grad_layout = (grad_pre[0] + grad_pre[1]).astype(jnp.bfloat16)
    table_terms = jnp.stack(
        [
            lax.dot_general(hot_x, grad_layout, contract_first, preferred_element_type=jnp.float32),
            lax.dot_general(hot_y, grad_layout, contract_first, preferred_element_type=jnp.float32),
        ]
    )
    table_rows = 2 * buckets
    tap_rows = 3 * kernel
    packed = jnp.concatenate(
        [
            table_terms.astype(jnp.bfloat16).reshape(table_rows, feat_width),
            tap_terms.astype(jnp.bfloat16).reshape(tap_rows, feat_width),
            gain_terms.astype(jnp.bfloat16).reshape(1, feat_width),
        ]
    )
    packed, layer_out, weight_parts = lax.optimization_barrier((packed, layer_out, weight_parts))
    summed = lax.psum(packed, "seq")
    summed = summed.astype(jnp.float32)
    weight_parts = lax.all_to_all(weight_parts, "seq", 0, 0, tiled=True)
    grad_weight = jnp.sum(weight_parts.astype(jnp.float32), axis=0)
    grad_tables = summed[:table_rows].reshape(2, buckets, feat_width)
    grad_taps = summed[table_rows : table_rows + tap_rows].reshape(3, kernel, feat_width)
    grad_gain = summed[table_rows + tap_rows]
    grad_query = grad_inputs[0].astype(jnp.bfloat16)
    grad_key = grad_inputs[1].astype(jnp.bfloat16)
    grad_value = grad_inputs[2].astype(jnp.bfloat16)
    return (
        layer_out,
        grad_query,
        grad_key,
        grad_value,
        grad_taps,
        grad_tables,
        grad_gain,
        grad_weight,
    )


def solution(mesh):
    return jax.shard_map(
        on_device,
        mesh=mesh,
        in_specs=(
            P("seq", "tp"),
            P("seq", "tp"),
            P("seq", "tp"),
            P(None, None, "tp"),
            P(None, "seq"),
            P(None, None, "tp"),
            P("tp", "seq"),
            P("tp"),
            P("tp", "seq"),
            P("seq", "tp"),
        ),
        out_specs=(
            P("seq", "tp"),
            P("seq", "tp"),
            P("seq", "tp"),
            P("seq", "tp"),
            P(None, None, "tp"),
            P(None, None, "tp"),
            P("tp"),
            P("tp", "seq"),
        ),
        check_vma=False,
    )
```

```python
import jax
import jax.numpy as jnp
from jax import lax
from jax.sharding import PartitionSpec as P

HIGHEST = lax.Precision.HIGHEST


def shifted(x, axis, by):
    length = lax.axis_size(axis)
    pairs = [(i, i + by) for i in range(length) if 0 <= i + by < length]
    return lax.ppermute(x, axis, pairs)


def exchanged(log_total, state, axis, by):
    heads, rows, cols = state.shape
    high = log_total.astype(jnp.bfloat16)
    low = (log_total - high.astype(jnp.float32)).astype(jnp.bfloat16)
    message = jnp.concatenate(
        [
            state.astype(jnp.bfloat16),
            jnp.broadcast_to(high[:, None, None], (heads, 8, cols)),
            jnp.broadcast_to(low[:, None, None], (heads, 8, cols)),
        ],
        axis=1,
    )
    message = shifted(message, axis, by).astype(jnp.float32)
    return message[:, rows, 0] + message[:, rows + 8, 0], message[:, :rows, :]


def entering(log_total, state, axis, reverse):
    length = lax.axis_size(axis)
    step = -1 if reverse else 1
    near_total, near_state = exchanged(log_total, state, axis, step)
    far_total, far_state = exchanged(log_total, state, axis, 2 * step)
    state = jnp.exp(near_total)[:, None, None] * far_state + near_state
    log_total = far_total + near_total
    distance = 2
    while distance < length:
        far_total, far_state = exchanged(log_total, state, axis, step * distance)
        state = jnp.exp(log_total)[:, None, None] * far_state + state
        log_total = far_total + log_total
        distance *= 2
    return state


def on_device(
    query_raw,
    key_raw,
    value_raw,
    conv_taps,
    layout_boxes,
    box_tables,
    log_decay,
    norm_gain,
    out_weight,
    grad_output,
):
    row_count, feat_width = query_raw.shape
    head_count = log_decay.shape[0]
    head_size = feat_width // head_count
    kernel = conv_taps.shape[1]
    buckets = box_tables.shape[1]
    feature_scale = head_size ** (-0.5)
    stacked = jnp.stack([query_raw, key_raw, value_raw])
    rim_rows = shifted(stacked[:, row_count - (kernel - 1) :, :], "seq", 1)
    padded = jnp.concatenate([rim_rows, stacked], axis=1).astype(jnp.float32)
    conved = jnp.zeros((3, row_count, feat_width), jnp.float32)
    for tap_step in range(kernel):
        conved = (
            conved
            + conv_taps[:, tap_step, None, :]
            * padded[:, kernel - 1 - tap_step : kernel - 1 - tap_step + row_count, :]
        )
    bucket_ids = jnp.arange(buckets, dtype=jnp.int32)

    def count_table(first, second):
        return (first[:, None] == bucket_ids[None, :]).astype(jnp.bfloat16) + (
            second[:, None] == bucket_ids[None, :]
        ).astype(jnp.bfloat16)

    hot_x = count_table(layout_boxes[0], layout_boxes[2])
    hot_y = count_table(layout_boxes[1], layout_boxes[3])
    layout = jnp.dot(hot_x, box_tables[0], preferred_element_type=jnp.float32) + jnp.dot(
        hot_y, box_tables[1], preferred_element_type=jnp.float32
    )
    query_feat = (feature_scale * (conved[0] + layout)).astype(jnp.bfloat16)
    key_feat = (conved[1] + layout).astype(jnp.bfloat16)
    value_feat = conved[2].astype(jnp.bfloat16)

    def split_heads(matrix):
        return matrix.reshape(row_count, head_count, head_size).transpose(1, 0, 2)

    def join_heads(blocks):
        return blocks.transpose(1, 0, 2).reshape(row_count, feat_width)

    query_heads = split_heads(query_feat)
    key_heads = split_heads(key_feat)
    value_heads = split_heads(value_feat)
    decay_sum = jnp.cumsum(log_decay, axis=1)
    decay_total = decay_sum[:, -1]
    head_decay = jnp.exp(decay_sum)[:, :, None]
    tail_decay = jnp.exp(decay_total[:, None] - decay_sum)[:, :, None]
    positions = jnp.arange(row_count, dtype=jnp.int32)
    causal_mask = positions[:, None] >= positions[None, :]
    decay_mask = jnp.where(
        causal_mask[None],
        jnp.exp(jnp.minimum(decay_sum[:, :, None] - decay_sum[:, None, :], 0.0)),
        0.0,
    )
    local_state = jnp.einsum("hsi,hsj->hij", key_heads * tail_decay, value_heads, precision=HIGHEST)
    incoming = entering(decay_total, local_state, "seq", False)
    scores = decay_mask * jnp.einsum(
        "hti,hsi->hts", query_heads, key_heads, preferred_element_type=jnp.float32
    )
    attended = jnp.einsum("hts,hsj->htj", scores, value_heads, precision=HIGHEST)
    attended = attended + head_decay * jnp.einsum(
        "hti,hij->htj", query_heads, incoming, precision=HIGHEST
    )
    inverse = lax.rsqrt(jnp.mean(attended * attended, axis=-1, keepdims=True) + 1e-06)
    unit_norm = attended * inverse
    gain_heads = norm_gain.reshape(head_count, 1, head_size)
    normed = join_heads(unit_norm * gain_heads).astype(jnp.bfloat16)
    partial_sum = jnp.dot(
        normed,
        lax.all_gather(out_weight, "seq", axis=1, tiled=True),
        preferred_element_type=jnp.float32,
    )
    layer_out = lax.psum_scatter(
        partial_sum.astype(jnp.bfloat16), "tp", scatter_dimension=1, tiled=True
    )
    cotangent = lax.all_gather(grad_output, "tp", axis=1, tiled=True)
    contract_last = (((1,), (1,)), ((), ()))
    grad_normed_sum = lax.dot_general(
        cotangent,
        lax.all_gather(out_weight, "seq", axis=1, tiled=True),
        contract_last,
        preferred_element_type=jnp.float32,
    )
    grad_normed = grad_normed_sum.astype(jnp.bfloat16)
    contract_first = (((0,), (0,)), ((), ()))
    weight_terms = lax.dot_general(
        normed, cotangent, contract_first, preferred_element_type=jnp.float32
    )
    grad_heads = split_heads(grad_normed).astype(jnp.float32)
    gain_terms = jnp.sum(grad_heads * unit_norm, axis=1).reshape(feat_width)
    grad_unit = grad_heads * gain_heads
    grad_attended = inverse * (
        grad_unit - unit_norm * jnp.mean(grad_unit * unit_norm, axis=-1, keepdims=True)
    )
    back_state = jnp.einsum(
        "hti,htj->hij", query_heads * head_decay, grad_attended, precision=HIGHEST
    )
    later_state = entering(decay_total, back_state, "seq", True)
    seq_count = lax.axis_size("seq")
    col_block = weight_terms.shape[1] // seq_count
    weight_parts = (
        weight_terms.astype(jnp.bfloat16)
        .reshape(feat_width, seq_count, col_block)
        .transpose(1, 0, 2)
    )
    weight_parts, later_state = lax.optimization_barrier((weight_parts, later_state))
    grad_scores = decay_mask * jnp.einsum(
        "htj,hsj->hts", grad_attended, value_heads, precision=HIGHEST
    )
    grad_qh = jnp.einsum(
        "hts,hsi->hti", grad_scores, key_heads, precision=HIGHEST
    ) + head_decay * jnp.einsum("htj,hij->hti", grad_attended, incoming, precision=HIGHEST)
    grad_kh = jnp.einsum(
        "hts,hti->hsi", grad_scores, query_heads, precision=HIGHEST
    ) + tail_decay * jnp.einsum("hsj,hij->hsi", value_heads, later_state, precision=HIGHEST)
    grad_vh = jnp.einsum(
        "hts,htj->hsj", scores, grad_attended, precision=HIGHEST
    ) + tail_decay * jnp.einsum("hsi,hij->hsj", key_heads, later_state, precision=HIGHEST)
    grad_pre = jnp.stack(
        [feature_scale * join_heads(grad_qh), join_heads(grad_kh), join_heads(grad_vh)]
    )
    next_rows = shifted(grad_pre[:, : kernel - 1, :], "seq", -1)
    extended = jnp.concatenate([grad_pre, next_rows], axis=1)
    grad_inputs = jnp.zeros((3, row_count, feat_width), jnp.float32)
    for tap_step in range(kernel):
        grad_inputs = (
            grad_inputs
            + conv_taps[:, tap_step, None, :] * extended[:, tap_step : tap_step + row_count, :]
        )
    tap_terms = jnp.stack(
        [
            jnp.sum(
                grad_pre * padded[:, kernel - 1 - tap_step : kernel - 1 - tap_step + row_count, :],
                axis=1,
            )
            for tap_step in range(kernel)
        ],
        axis=1,
    )
    grad_layout = (grad_pre[0] + grad_pre[1]).astype(jnp.bfloat16)
    table_terms = jnp.stack(
        [
            lax.dot_general(hot_x, grad_layout, contract_first, preferred_element_type=jnp.float32),
            lax.dot_general(hot_y, grad_layout, contract_first, preferred_element_type=jnp.float32),
        ]
    )
    table_rows = 2 * buckets
    tap_rows = 3 * kernel
    packed = jnp.concatenate(
        [
            table_terms.astype(jnp.bfloat16).reshape(table_rows, feat_width),
            tap_terms.astype(jnp.bfloat16).reshape(tap_rows, feat_width),
            gain_terms.astype(jnp.bfloat16).reshape(1, feat_width),
        ]
    )
    packed, layer_out, weight_parts = lax.optimization_barrier((packed, layer_out, weight_parts))
    summed = lax.psum(packed, "seq")
    summed = summed.astype(jnp.float32)
    weight_parts = lax.all_to_all(weight_parts, "seq", 0, 0, tiled=True)
    grad_weight = jnp.sum(weight_parts.astype(jnp.float32), axis=0)
    grad_tables = summed[:table_rows].reshape(2, buckets, feat_width)
    grad_taps = summed[table_rows : table_rows + tap_rows].reshape(3, kernel, feat_width)
    grad_gain = summed[table_rows + tap_rows]
    grad_query = grad_inputs[0].astype(jnp.bfloat16)
    grad_key = grad_inputs[1].astype(jnp.bfloat16)
    grad_value = grad_inputs[2].astype(jnp.bfloat16)
    return (
        layer_out,
        grad_query,
        grad_key,
        grad_value,
        grad_taps,
        grad_tables,
        grad_gain,
        grad_weight,
    )


def solution(mesh):
    return jax.shard_map(
        on_device,
        mesh=mesh,
        in_specs=(
            P("seq", "tp"),
            P("seq", "tp"),
            P("seq", "tp"),
            P(None, None, "tp"),
            P(None, "seq"),
            P(None, None, "tp"),
            P("tp", "seq"),
            P("tp"),
            P("tp", "seq"),
            P("seq", "tp"),
        ),
        out_specs=(
            P("seq", "tp"),
            P("seq", "tp"),
            P("seq", "tp"),
            P("seq", "tp"),
            P(None, None, "tp"),
            P(None, None, "tp"),
            P("tp"),
            P("tp", "seq"),
        ),
        check_vma=False,
    )
```
